32 devices in a mesh: lon: 8 (over z, x), lat: 4 (over y, core).
Axes of the slice: x: 2, y: 2, z: 4, core: 2. Of those that a mesh axis runs over, the one named last changes fastest.
Arguments:
- thermal_departure: float32 [90, 128, 1024], P(None, 'lat', 'lon'), may hold values from -6 to 6
- moisture_profile: float32 [90, 128, 1024], P(None, 'lat', 'lon'), may hold values from -6 to 6
- solar_elevation_factor: float32 [128, 1024], P('lat', 'lon'), may hold values from 0.1 to 1
- daylight_groups: int32 [128, 8], P('lat', 'lon'), may hold values from 0 to 1, as said below
- spreading_factor: float32 [128, 1024], P('lat', 'lon'), may hold values from 0.03 to 0.24
- entry_layer_matrix: float32 [512, 181], replicated, may hold values from -0.4375 to 0.4375
- entry_layer_offset: float32 [512], replicated, may hold values from -3 to 3
- inner_layer_matrices: float32 [2, 512, 512], replicated, may hold values from -0.25 to 0.25
- inner_layer_offsets: float32 [2, 512], replicated, may hold values from -3 to 3
- final_layer_matrix: float32 [90, 512], replicated, may hold values from -0.25 to 0.25
- final_layer_offset: float32 [90], replicated, may hold values from -3 to 3
Outputs:
- heating: float32 [90, 128, 1024], P(None, 'lat', 'lon')
- temp_next: float32 [90, 128, 1024], P(None, 'lat', 'lon')
The draws below stay inside these ranges and needn't reach their ends.
Inputs may be any that keep to these rules, and one draw needn't show every extreme that they name: In every row the sunlit strips form one run of 4 consecutive strips, wrapping around, so daylight_groups[r, j] + daylight_groups[r, (j + 4) mod 8] == 1; row r and row r + 32 are complements of each other.
All inputs are finite; a program needn't handle non-finite values.
Results may differ from the reference program's by a relative error of at most 0.0001.
Values sent between devices are 32-bit elements; how exact they have to be, the bound alone decides.
A program may use at most 64 MiB of HBM per device.

```python
import math
import jax
import jax.numpy as jnp
from jax import lax

ALTITUDE_TIERS = 90
HID = 512
DEPTH = 2
BLOCK = 128
NB = 32
STEPS = 2
FEAT = 181
MERIDIAN_SPAN = 128
ZONAL_SPAN = 1024
STRIPS = 8


def draw_daylight_groups(key, part):
    key_base = jax.random.fold_in(key, 11)
    key_jitter = jax.random.fold_in(key, 23)
    base = jax.random.randint(key_base, (), 0, STRIPS)
    jitter_local = jax.random.randint(key_jitter, (NB,), -1, 2)
    row_index = jnp.arange(MERIDIAN_SPAN, dtype=jnp.int32)
    band_flip = jnp.mod(row_index // NB, 2) * (STRIPS // 2)
    jitter = jitter_local[jnp.mod(row_index, NB)] + band_flip
    strip = jnp.arange(STRIPS, dtype=jnp.int32)
    offset = jnp.mod(strip[None, :] - base - jitter[:, None], STRIPS)
    return jnp.where(offset < STRIPS // 2, 1, 0).astype(jnp.int32)


def block_scale(key, extent, pieces, low, top_value):
    loudness = 1.0
    for position, blocks in pieces:
        steps = jax.random.uniform(jax.random.fold_in(jax.random.fold_in(key, 6), position), (blocks,), jnp.float32, low / len(pieces), top_value / len(pieces))
        loudness = loudness * jnp.repeat(jnp.exp(steps), extent[position] // blocks).reshape((-1,) + (1,) * (len(extent) - 1 - position))
    return loudness


def bell_draw(own_key, shape, spread, reach, split=(), held_as=jnp.bfloat16):
    values = spread * jax.random.normal(own_key, shape, jnp.float32)
    if split:
        values = values * block_scale(own_key, shape, split, -0.22, 0.18)
    return jnp.clip(values, -reach, reach).astype(held_as)


def setup_inputs(seed: int = 0) -> dict:
    seeds = jax.random.split(jax.random.key(seed), 12)
    return {
        "thermal_departure": bell_draw(seeds[0], (ALTITUDE_TIERS, MERIDIAN_SPAN, ZONAL_SPAN), 1.0, 6.0, ((1, 4), (2, 8)), jnp.float32),
        "moisture_profile": bell_draw(seeds[1], (ALTITUDE_TIERS, MERIDIAN_SPAN, ZONAL_SPAN), 1.0, 6.0, ((1, 4), (2, 8)), jnp.float32),
        "solar_elevation_factor": jnp.clip(0.1 + 0.9 * jax.random.uniform(seeds[2], (MERIDIAN_SPAN, ZONAL_SPAN), jnp.float32) ** block_scale(seeds[2], (MERIDIAN_SPAN, ZONAL_SPAN), ((0, 4), (1, 8)), -0.2, 0.2), 0.1, 1.0),
        "daylight_groups": draw_daylight_groups(jax.random.fold_in(seeds[11], 71), 0),
        "spreading_factor": jnp.clip(jnp.exp(math.log(0.24) - 2.0794415 * jax.random.uniform(seeds[4], (MERIDIAN_SPAN, ZONAL_SPAN), jnp.float32) ** block_scale(seeds[4], (MERIDIAN_SPAN, ZONAL_SPAN), ((0, 4), (1, 8)), -0.2, 0.2)), 0.03, 0.24),
        "entry_layer_matrix": bell_draw(seeds[5], (HID, FEAT), FEAT ** -0.5, 0.4375, (), jnp.float32),
        "entry_layer_offset": bell_draw(seeds[6], (HID,), 0.5, 3.0, (), jnp.float32),
        "inner_layer_matrices": bell_draw(seeds[7], (DEPTH, HID, HID), HID ** -0.5, 0.25, (), jnp.float32),
        "inner_layer_offsets": bell_draw(seeds[8], (DEPTH, HID), 0.5, 3.0, (), jnp.float32),
        "final_layer_matrix": bell_draw(seeds[9], (ALTITUDE_TIERS, HID), HID ** -0.5, 0.25, (), jnp.float32),
        "final_layer_offset": bell_draw(seeds[10], (ALTITUDE_TIERS,), 0.5, 3.0, (), jnp.float32),
    }


def network_apply(columns, entry_layer_matrix, entry_layer_offset, inner_layer_matrices, inner_layer_offsets, final_layer_matrix, final_layer_offset):
    hidden = jax.nn.silu(jnp.dot(entry_layer_matrix, columns, precision=lax.Precision.HIGHEST) + entry_layer_offset[:, None])
    for layer in range(DEPTH):
        hidden = jax.nn.silu(jnp.dot(inner_layer_matrices[layer], hidden, precision=lax.Precision.HIGHEST) + inner_layer_offsets[layer][:, None])
    return jnp.dot(final_layer_matrix, hidden, precision=lax.Precision.HIGHEST) + final_layer_offset[:, None]


def diffuse(atmosphere_snapshot, spreading_factor):
    padded = jnp.concatenate([atmosphere_snapshot[:, :, -1:], atmosphere_snapshot, atmosphere_snapshot[:, :, :1]], axis=2)
    padded = jnp.pad(padded, ((0, 0), (1, 1), (0, 0)))
    beside_all = padded[:, :-2, 1:-1] + padded[:, 2:, 1:-1] + padded[:, 1:-1, :-2] + padded[:, 1:-1, 2:]
    return atmosphere_snapshot + spreading_factor[None] * (beside_all - 4.0 * atmosphere_snapshot)


def reference(thermal_departure, moisture_profile, solar_elevation_factor, daylight_groups, spreading_factor, entry_layer_matrix, entry_layer_offset, inner_layer_matrices, inner_layer_offsets, final_layer_matrix, final_layer_offset):
    thermal_tracks = jnp.moveaxis(thermal_departure, 1, 0)
    moisture_tracks = jnp.moveaxis(moisture_profile, 1, 0)

    def single_parallel(packed):
        temp_row, humid_row, cos_row, lit_row = packed
        columns = jnp.concatenate([temp_row, humid_row, cos_row[None]], axis=0)
        output = network_apply(columns, entry_layer_matrix, entry_layer_offset, inner_layer_matrices, inner_layer_offsets, final_layer_matrix, final_layer_offset)
        lit_cols = jnp.repeat(lit_row.astype(jnp.float32), BLOCK)
        return output * (cos_row * lit_cols)[None]

    warming_tracks = lax.map(single_parallel, (thermal_tracks, moisture_tracks, solar_elevation_factor, daylight_groups))
    heating = jnp.moveaxis(warming_tracks, 0, 1)
    atmosphere_snapshot = thermal_departure
    for substep in range(STEPS):
        atmosphere_snapshot = diffuse(atmosphere_snapshot, spreading_factor)
    return heating, atmosphere_snapshot + heating
```

```python
import functools

import jax
import jax.numpy as jnp
from jax import lax
from jax.experimental import pallas as pl
from jax.experimental.pallas import tpu as pltpu
from jax.sharding import PartitionSpec as P

STEPS = 2
MESH = pl.DeviceIdType.MESH
GROUP = 4


def padded_2(block, sides, width):
    for axis, dim in sides:
        count = lax.axis_size(axis)
        forward = [(i, i + 1) for i in range(count - 1)]
        forward.append((count - 1, 0))
        backward = [(target, source) for source, target in forward]
        low = lax.ppermute(
            lax.slice_in_dim(block, block.shape[dim] - width, None, axis=dim), axis, forward
        )
        high = lax.ppermute(lax.slice_in_dim(block, 0, width, axis=dim), axis, backward)
        block = jnp.concatenate([low, block, high], axis=dim)
    return block


def up8(n):
    return (n + 7) // 8 * 8


def split(x):
    hi = x.astype(jnp.bfloat16)
    lo = (x - hi.astype(jnp.float32)).astype(jnp.bfloat16)
    return hi, lo


def dot(a, b):
    return jnp.dot(a, b, preferred_element_type=jnp.float32)


def dot3(w_hi, w_lo, x):
    hi, lo = split(x)
    return dot(w_hi, hi) + dot(w_hi, lo) + dot(w_lo, hi)


def gate(h):
    return h + h * jnp.tanh(h)


def net_kernel(
    temp, moist, mu, lit, w0t, b0, wm, bm, wf, bf,
    heat,
    temp_v, moist_v, mu_v, temp_r, moist_r, mu_r,
    w0_hi, w0_lo, wm_hi, wm_lo, wf_hi, wf_lo, b0_c, bm_c, bf_c,
    xs, res, res_r,
    in_sem, send_sem, recv_sem, out_send, out_recv,
):
    levels, rows, lanes = temp.shape
    half = rows // 2
    hid = wm.shape[1]
    depth = wm.shape[0]
    lp = up8(levels)
    lat = lax.axis_index("lat")
    parity = lax.rem(lat, 2)
    partner = lat + 1 - 2 * parity
    mine = pl.multiple_of(parity * half, half)
    theirs = pl.multiple_of(half - parity * half, half)

    own = [
        pltpu.make_async_copy(temp, temp_v, in_sem.at[0]),
        pltpu.make_async_copy(moist, moist_v, in_sem.at[1]),
        pltpu.make_async_copy(mu, mu_v, in_sem.at[2]),
    ]
    for copy in own:
        copy.start()

    barrier = pltpu.get_barrier_semaphore()
    pl.semaphore_signal(barrier, inc=1, device_id={"lat": partner}, device_id_type=MESH)
    pl.semaphore_wait(barrier, 1)

    out = [
        pltpu.make_async_remote_copy(
            src_ref=src, dst_ref=dst, send_sem=send_sem.at[i], recv_sem=recv_sem.at[i],
            device_id={"lat": partner}, device_id_type=MESH)
        for i, (src, dst) in enumerate((
            (temp.at[:, pl.ds(theirs, half), :], temp_r),
            (moist.at[:, pl.ds(theirs, half), :], moist_r),
            (mu.at[pl.ds(theirs, half), :], mu_r),
        ))
    ]
    for copy in out:
        copy.start()

    kp = xs.shape[0]
    xs[...] = jnp.zeros_like(xs)
    xs[0:levels, 0:hid] = w0t[0:levels, :] * 0.5
    xs[lp:lp + levels, 0:hid] = w0t[levels:2 * levels, :] * 0.5
    xs[2 * lp:2 * lp + 1, 0:hid] = w0t[2 * levels:2 * levels + 1, :] * 0.5
    w0_hi[...], w0_lo[...] = split(xs[:, 0:hid].T)
    for k in range(depth):
        wm_hi[k], wm_lo[k] = split(wm[k] * 0.5)
    wf_hi[...], wf_lo[...] = split(wf[...])

    def column(row):
        return jnp.broadcast_to(row, (lanes, row.shape[1])).T

    b0_c[...] = column(b0[...] * 0.5)
    for k in range(depth):
        bm_c[k] = column(bm[k:k + 1, :] * 0.5)
    bf_c[...] = column(bf[...])
    xs[...] = jnp.zeros_like(xs)

    for copy in own:
        copy.wait()
    for copy in out:
        copy.wait()

    temp_f = temp_v.reshape(levels * rows, lanes)
    moist_f = moist_v.reshape(levels * rows, lanes)
    temp_rf = temp_r.reshape(levels * half, lanes)
    moist_rf = moist_r.reshape(levels * half, lanes)

    def wide(c):
        return jnp.concatenate([c] * GROUP, axis=1)

    def send(g):
        rows_g = pl.ds(g * GROUP, GROUP)
        return pltpu.make_async_remote_copy(
            src_ref=res.at[rows_g], dst_ref=res_r.at[rows_g],
            send_sem=out_send.at[g], recv_sem=out_recv.at[g],
            device_id={"lat": partner}, device_id_type=MESH)

    def step(g, carry):
        for j in range(GROUP):
            i = g * GROUP + j
            r = mine + i
            on = lit[r].astype(jnp.float32)
            off = 1.0 - on
            cols = slice(j * lanes, (j + 1) * lanes)
            xs[0:levels, cols] = (
                temp_f[pl.ds(r, levels, stride=rows), :] * on
                + temp_rf[pl.ds(i, levels, stride=half), :] * off)
            xs[lp:lp + levels, cols] = (
                moist_f[pl.ds(r, levels, stride=rows), :] * on
                + moist_rf[pl.ds(i, levels, stride=half), :] * off)
            xs[2 * lp:2 * lp + 1, cols] = (
                mu_v[pl.ds(r, 1), :] * on + mu_r[pl.ds(i, 1), :] * off)
        h = gate(dot3(w0_hi[...], w0_lo[...], xs[...]) + wide(b0_c[...]))
        for k in range(depth):
            h = gate(dot3(wm_hi[k], wm_lo[k], h) + wide(bm_c[k]))
        y = dot3(wf_hi[...], wf_lo[...], h) + wide(bf_c[...])
        y = y * xs[2 * lp:2 * lp + 1, :]
        for j in range(GROUP):
            res[g * GROUP + j] = y[:, j * lanes:(j + 1) * lanes]
        send(g).start()
        return carry

    lax.fori_loop(0, half // GROUP, step, 0)

    heat_f = heat.reshape(levels * rows, lanes)
    for i in range(half):
        r = mine + i
        heat_f[pl.ds(r, levels, stride=rows), :] = res[i] * lit[r].astype(jnp.float32)
    for g in range(half // GROUP):
        send(g).wait()
    for i in range(half):
        r = theirs + i
        heat_f[pl.ds(r, levels, stride=rows), :] = res_r[i] * lit[r].astype(jnp.float32)


def radiate(temp, moist, mu, lit, w0, b0, wm, bm, wf, bf):
    levels, rows, lanes = temp.shape
    half = rows // 2
    hid = wm.shape[1]
    depth = wm.shape[0]
    lp = up8(levels)
    kp = 256
    while kp < 2 * lp + 1:
        kp += 256
    f32, bf16 = jnp.float32, jnp.bfloat16
    vmem = pl.BlockSpec(memory_space=pltpu.VMEM)
    any_ = pl.BlockSpec(memory_space=pl.ANY)
    groups = half // GROUP
    return pl.pallas_call(
        net_kernel,
        out_shape=jax.ShapeDtypeStruct((levels, rows, lanes), f32),
        in_specs=[any_, any_, any_, pl.BlockSpec(memory_space=pltpu.SMEM)] + [vmem] * 6,
        out_specs=vmem,
        scratch_shapes=[
            pltpu.VMEM((levels, rows, lanes), f32),
            pltpu.VMEM((levels, rows, lanes), f32),
            pltpu.VMEM((rows, lanes), f32),
            pltpu.VMEM((levels, half, lanes), f32),
            pltpu.VMEM((levels, half, lanes), f32),
            pltpu.VMEM((half, lanes), f32),
            pltpu.VMEM((hid, kp), bf16),
            pltpu.VMEM((hid, kp), bf16),
            pltpu.VMEM((depth, hid, hid), bf16),
            pltpu.VMEM((depth, hid, hid), bf16),
            pltpu.VMEM((levels, hid), bf16),
            pltpu.VMEM((levels, hid), bf16),
            pltpu.VMEM((hid, lanes), f32),
            pltpu.VMEM((depth, hid, lanes), f32),
            pltpu.VMEM((levels, lanes), f32),
            pltpu.VMEM((kp, max(hid, GROUP * lanes)), f32),
            pltpu.VMEM((half, levels, lanes), f32),
            pltpu.VMEM((half, levels, lanes), f32),
            pltpu.SemaphoreType.DMA((3,)),
            pltpu.SemaphoreType.DMA((3,)),
            pltpu.SemaphoreType.DMA((3,)),
            pltpu.SemaphoreType.DMA((groups,)),
            pltpu.SemaphoreType.DMA((groups,)),
        ],
        compiler_params=pltpu.CompilerParams(
            collective_id=0, has_side_effects=True, vmem_limit_bytes=48 << 20),
    )(temp, moist, mu, lit, w0.T, b0[None, :], wm, bm, wf, bf[None, :])


def on_device(
    thermal_departure,
    moisture_profile,
    solar_elevation_factor,
    daylight_groups,
    spreading_factor,
    entry_layer_matrix,
    entry_layer_offset,
    inner_layer_matrices,
    inner_layer_offsets,
    final_layer_matrix,
    final_layer_offset,
):
    lat_index = lax.axis_index("lat")
    lat_first = lat_index == 0
    lat_last = lat_index == lax.axis_size("lat") - 1
    atmosphere_snapshot = thermal_departure
    for substep in range(STEPS):
        padded = padded_2(atmosphere_snapshot, (("lon", 2), ("lat", 1)), 1)
        padded = padded.at[:, 0, :].multiply(jnp.where(lat_first, 0.0, 1.0))
        padded = padded.at[:, -1, :].multiply(jnp.where(lat_last, 0.0, 1.0))
        beside_all = (
            padded[:, :-2, 1:-1] + padded[:, 2:, 1:-1] + padded[:, 1:-1, :-2] + padded[:, 1:-1, 2:]
        )
        atmosphere_snapshot = atmosphere_snapshot + spreading_factor[None] * (
            beside_all - 4.0 * atmosphere_snapshot
        )
    heating = radiate(
        thermal_departure,
        moisture_profile,
        solar_elevation_factor,
        daylight_groups[:, 0],
        entry_layer_matrix,
        entry_layer_offset,
        inner_layer_matrices,
        inner_layer_offsets,
        final_layer_matrix,
        final_layer_offset,
    )
    return (heating, atmosphere_snapshot + heating)


def solution(mesh):
    in_specs = (
        P(None, "lat", "lon"),
        P(None, "lat", "lon"),
        P("lat", "lon"),
        P("lat", "lon"),
        P("lat", "lon"),
        P(),
        P(),
        P(),
        P(),
        P(),
        P(),
    )
    out_specs = (P(None, "lat", "lon"), P(None, "lat", "lon"))
    return jax.shard_map(
        on_device, mesh=mesh, in_specs=in_specs, out_specs=out_specs, check_vma=False
    )
```

```python
import jax
import jax.numpy as jnp
from jax import lax
from jax.experimental import pallas as pl
from jax.experimental.pallas import tpu as pltpu
from jax.sharding import PartitionSpec as P

MESH = pl.DeviceIdType.MESH
GROUP = 4
EDGE = 4
PAD = 8


def up8(n):
    return (n + 7) // 8 * 8


def split(x):
    hi = x.astype(jnp.bfloat16)
    lo = (x - hi.astype(jnp.float32)).astype(jnp.bfloat16)
    return hi, lo


def dot(a, b):
    return jnp.dot(a, b, preferred_element_type=jnp.float32)


def dot3(w_hi, w_lo, x):
    hi, lo = split(x)
    return dot(w_hi, hi) + dot(w_hi, lo) + dot(w_lo, hi)


def gate(h):
    return h + h * jnp.tanh(h)


def roll(x, shift, axis):
    return pltpu.roll(x, shift % x.shape[axis], axis)


def kernel(
    temp, moist, mu, lit, spread, w0t, b0, wm, bm, wf, bf,
    heat, nxt,
    temp_v, moist_v, mu_v, spread_v, temp_r, moist_r, mu_r,
    w0_hi, w0_lo, wm_hi, wm_lo, wf_hi, wf_lo, b0_c, bm_c, bf_c,
    xs, res, res_r,
    temp_t, temp_b, spread_t, spread_b,
    pack, left_m, left_t, left_b, right_m, right_t, right_b,
    edge_0, edge_1,
    in_sem, send_sem, recv_sem, out_send, out_recv, halo_send, halo_recv,
):
    levels, rows, lanes = temp.shape
    half = rows // 2
    hid = wm.shape[1]
    depth = wm.shape[0]
    lp = up8(levels)
    tiles = pack.shape[0] - 1
    slots = lanes // EDGE
    n_lat = lax.axis_size("lat")
    n_lon = lax.axis_size("lon")
    lat = lax.axis_index("lat")
    lon = lax.axis_index("lon")
    parity = lax.rem(lat, 2)
    partner = lat + 1 - 2 * parity
    mine = pl.multiple_of(parity * half, half)
    theirs = pl.multiple_of(half - parity * half, half)
    left = lax.rem(lon + n_lon - 1, n_lon)
    right = lax.rem(lon + 1, n_lon)
    has_up = lat > 0
    has_down = lat < n_lat - 1
    up = jnp.maximum(lat - 1, 0)
    down = jnp.minimum(lat + 1, n_lat - 1)

    own = [
        pltpu.make_async_copy(src, dst, in_sem.at[i])
        for i, (src, dst) in enumerate((
            (temp, temp_v), (moist, moist_v), (mu, mu_v), (spread, spread_v)))
    ]
    for copy in own:
        copy.start()

    def at(lat_to, lon_to):
        return {"lat": lat_to, "lon": lon_to}

    barrier = pltpu.get_barrier_semaphore()

    def hello(lat_to, lon_to):
        pl.semaphore_signal(barrier, inc=1, device_id=at(lat_to, lon_to), device_id_type=MESH)

    hello(lat, left)
    hello(lat, right)

    @pl.when(has_up)
    def _():
        for to in (left, lon, right):
            hello(up, to)

    @pl.when(has_down)
    def _():
        for to in (left, lon, right):
            hello(down, to)

    pl.semaphore_wait(
        barrier, 2 + 3 * has_up.astype(jnp.int32) + 3 * has_down.astype(jnp.int32))

    out = [
        pltpu.make_async_remote_copy(
            src_ref=src, dst_ref=dst, send_sem=send_sem.at[i], recv_sem=recv_sem.at[i],
            device_id=at(partner, lon), device_id_type=MESH)
        for i, (src, dst) in enumerate((
            (mu.at[pl.ds(theirs, half), :], mu_r),
            (temp.at[:, pl.ds(theirs, half), :], temp_r),
            (moist.at[:, pl.ds(theirs, half), :], moist_r),
        ))
    ]
    for copy in out:
        copy.start()

    first, last = pl.ds(0, PAD), pl.ds(rows - PAD, PAD)

    def halo(i, src, dst, lat_to, lon_to):
        return pltpu.make_async_remote_copy(
            src_ref=src, dst_ref=dst, send_sem=halo_send.at[i], recv_sem=halo_recv.at[i],
            device_id=at(lat_to, lon_to), device_id_type=MESH)

    beside = [
        halo(0, pack, right_m, lat, left),
        halo(1, pack, left_m, lat, right),
    ]
    to_up = [
        halo(2, spread.at[first, :], spread_b, up, lon),
        halo(3, temp.at[:, first, :], temp_b, up, lon),
        halo(4, pack.at[:, first, :], right_b, up, left),
        halo(5, pack.at[:, first, :], left_b, up, right),
    ]
    to_down = [
        halo(6, spread.at[last, :], spread_t, down, lon),
        halo(7, temp.at[:, last, :], temp_t, down, lon),
        halo(8, pack.at[:, last, :], right_t, down, left),
        halo(9, pack.at[:, last, :], left_t, down, right),
    ]

    for copy in (own[0], own[3], own[2]):
        copy.wait()
    lane = lax.broadcasted_iota(jnp.int32, (rows, lanes), 1)
    for t in range(tiles):
        count = min(slots, levels - t * slots)
        acc = jnp.zeros((rows, lanes), jnp.float32)
        for m in range(count):
            moved = roll(temp_v[t * slots + m], EDGE * m + 2, 1)
            acc = jnp.where(lane // EDGE == m, moved, acc)
        pack[t] = acc
    acc = jnp.where(lane < EDGE, roll(spread_v[...], 2, 1), 0.0)
    step = EDGE
    while step < lanes:
        acc = acc + roll(acc, step, 1)
        step *= 2
    pack[tiles] = acc

    for copy in beside:
        copy.start()

    @pl.when(has_up)
    def _():
        for copy in to_up:
            copy.start()

    @pl.when(has_down)
    def _():
        for copy in to_down:
            copy.start()

    @pl.when(jnp.logical_not(has_up))
    def _():
        for ref in (temp_t, spread_t, left_t, right_t):
            ref[...] = jnp.zeros_like(ref)

    @pl.when(jnp.logical_not(has_down))
    def _():
        for ref in (temp_b, spread_b, left_b, right_b):
            ref[...] = jnp.zeros_like(ref)

    xs[...] = jnp.zeros_like(xs)
    xs[0:levels, 0:hid] = w0t[0:levels, :] * 0.5
    xs[lp:lp + levels, 0:hid] = w0t[levels:2 * levels, :] * 0.5
    xs[2 * lp:2 * lp + 1, 0:hid] = w0t[2 * levels:2 * levels + 1, :] * 0.5
    w0_hi[...], w0_lo[...] = split(xs[:, 0:hid].T)
    for k in range(depth):
        wm_hi[k], wm_lo[k] = split(wm[k] * 0.5)
    wf_hi[...], wf_lo[...] = split(wf[...])

    def column(row):
        return jnp.broadcast_to(row, (lanes, row.shape[1])).T

    b0_c[...] = column(b0[...] * 0.5)
    for k in range(depth):
        bm_c[k] = column(bm[k:k + 1, :] * 0.5)
    bf_c[...] = column(bf[...])
    xs[...] = jnp.zeros_like(xs)

    own[1].wait()
    for copy in out:
        copy.wait()

    temp_f = temp_v.reshape(levels * rows, lanes)
    moist_f = moist_v.reshape(levels * rows, lanes)
    temp_rf = temp_r.reshape(levels * half, lanes)
    moist_rf = moist_r.reshape(levels * half, lanes)

    def wide(c):
        return jnp.concatenate([c] * GROUP, axis=1)

    def send(g):
        rows_g = pl.ds(g * GROUP, GROUP)
        return pltpu.make_async_remote_copy(
            src_ref=res.at[rows_g], dst_ref=res_r.at[rows_g],
            send_sem=out_send.at[g], recv_sem=out_recv.at[g],
            device_id=at(partner, lon), device_id_type=MESH)

    def network(g, carry):
        for j in range(GROUP):
            i = g * GROUP + j
            r = mine + i
            on = lit[r].astype(jnp.float32)
            off = 1.0 - on
            cols = slice(j * lanes, (j + 1) * lanes)
            xs[0:levels, cols] = (
                temp_f[pl.ds(r, levels, stride=rows), :] * on
                + temp_rf[pl.ds(i, levels, stride=half), :] * off)
            xs[lp:lp + levels, cols] = (
                moist_f[pl.ds(r, levels, stride=rows), :] * on
                + moist_rf[pl.ds(i, levels, stride=half), :] * off)
            xs[2 * lp:2 * lp + 1, cols] = (
                mu_v[pl.ds(r, 1), :] * on + mu_r[pl.ds(i, 1), :] * off)
        h = gate(dot3(w0_hi[...], w0_lo[...], xs[...]) + wide(b0_c[...]))
        for k in range(depth):
            h = gate(dot3(wm_hi[k], wm_lo[k], h) + wide(bm_c[k]))
        y = dot3(wf_hi[...], wf_lo[...], h) + wide(bf_c[...])
        y = y * xs[2 * lp:2 * lp + 1, :]
        for j in range(GROUP):
            res[g * GROUP + j] = y[:, j * lanes:(j + 1) * lanes]
        send(g).start()
        return carry

    lax.fori_loop(0, half // GROUP, network, 0)

    for copy in beside:
        copy.wait()

    @pl.when(has_up)
    def _():
        for copy in to_up:
            copy.wait_send()
        for copy in to_down:
            copy.wait_recv()

    @pl.when(has_down)
    def _():
        for copy in to_down:
            copy.wait_send()
        for copy in to_up:
            copy.wait_recv()

    tall = rows + 2 * PAD

    def stack(top, middle, bottom):
        return jnp.concatenate([top, middle, bottom], axis=0)

    def advance(x, f, west, east):
        beside = roll(x, 1, 0) + roll(x, tall - 1, 0) + west + east
        return x + f * (beside - 4.0 * x)

    slot = lax.broadcasted_iota(jnp.int32, (tall, lanes), 1)
    place = lax.rem(slot, EDGE)
    zero8 = jnp.zeros((PAD, lanes), jnp.float32)

    def gather(t):
        lhs = stack(left_t[t], left_m[t], left_b[t])
        rhs = stack(right_t[t], right_m[t], right_b[t])
        here = stack(zero8, pack[t], zero8)
        return (jnp.where(place < 2, lhs, here), jnp.where(place < 2, here, rhs))

    f_west, f_east = gather(tiles)
    for t in range(tiles):
        west, east = gather(t)
        edge_0[t] = jnp.where(place == 1, roll(east, lanes - 1, 1), roll(west, 1, 1))
        west = advance(west, f_west, roll(west, 1, 1), roll(west, lanes - 1, 1))
        east = advance(east, f_east, roll(east, 1, 1), roll(east, lanes - 1, 1))
        edge_1[t] = jnp.where(place == 1, roll(east, lanes - 1, 1), roll(west, 1, 1))

    f_all = stack(spread_t[...], spread_v[...], spread_b[...])
    for k in range(levels):
        t, m = divmod(k, slots)
        turn = lanes - 2 - EDGE * m
        x = stack(temp_t[k], temp_v[k], temp_b[k])
        for edge in (edge_0, edge_1):
            rim = roll(edge[t], turn, 1)
            west = jnp.where(slot == 0, rim, roll(x, 1, 1))
            east = jnp.where(slot == lanes - 1, rim, roll(x, lanes - 1, 1))
            x = advance(x, f_all, west, east)
        nxt[k] = x[PAD:PAD + rows]

    heat_f = heat.reshape(levels * rows, lanes)
    nxt_f = nxt.reshape(levels * rows, lanes)

    def place_row(r, value):
        there = pl.ds(r, levels, stride=rows)
        value = value * lit[r].astype(jnp.float32)
        heat_f[there, :] = value
        nxt_f[there, :] = nxt_f[there, :] + value

    for i in range(half):
        place_row(mine + i, res[i])
    for g in range(half // GROUP):
        send(g).wait()
    for i in range(half):
        place_row(theirs + i, res_r[i])


def run(temp, moist, mu, lit, spread, w0, b0, wm, bm, wf, bf):
    levels, rows, lanes = temp.shape
    half = rows // 2
    hid = wm.shape[1]
    depth = wm.shape[0]
    lp = up8(levels)
    kp = (2 * lp + 256) // 256 * 256
    tall = rows + 2 * PAD
    tiles = (levels * EDGE + lanes - 1) // lanes
    f32, bf16 = jnp.float32, jnp.bfloat16
    vmem = pl.BlockSpec(memory_space=pltpu.VMEM)
    hbm = pl.BlockSpec(memory_space=pltpu.HBM)
    smem = pl.BlockSpec(memory_space=pltpu.SMEM)
    groups = half // GROUP
    dma = pltpu.SemaphoreType.DMA

    def buf(*shape, dtype=f32):
        return pltpu.VMEM(shape, dtype)

    return pl.pallas_call(
        kernel,
        out_shape=(jax.ShapeDtypeStruct(temp.shape, f32),) * 2,
        in_specs=[hbm, hbm, hbm, smem, hbm] + [vmem] * 6,
        out_specs=(vmem, vmem),
        scratch_shapes=[
            buf(levels, rows, lanes), buf(levels, rows, lanes), buf(rows, lanes), buf(rows, lanes),
            buf(levels, half, lanes), buf(levels, half, lanes), buf(half, lanes),
            buf(hid, kp, dtype=bf16), buf(hid, kp, dtype=bf16),
            buf(depth, hid, hid, dtype=bf16), buf(depth, hid, hid, dtype=bf16),
            buf(levels, hid, dtype=bf16), buf(levels, hid, dtype=bf16),
            buf(hid, lanes), buf(depth, hid, lanes), buf(levels, lanes),
            buf(kp, max(hid, GROUP * lanes)), buf(half, levels, lanes), buf(half, levels, lanes),
            buf(levels, PAD, lanes), buf(levels, PAD, lanes), buf(PAD, lanes), buf(PAD, lanes),
            buf(tiles + 1, rows, lanes),
            buf(tiles + 1, rows, lanes), buf(tiles + 1, PAD, lanes), buf(tiles + 1, PAD, lanes),
            buf(tiles + 1, rows, lanes), buf(tiles + 1, PAD, lanes), buf(tiles + 1, PAD, lanes),
            buf(tiles, tall, lanes), buf(tiles, tall, lanes),
            dma((4,)), dma((3,)), dma((3,)), dma((groups,)), dma((groups,)),
            dma((10,)), dma((10,)),
        ],
        compiler_params=pltpu.CompilerParams(
            collective_id=0, has_side_effects=True, vmem_limit_bytes=48 << 20),
    )(temp, moist, mu, lit, spread, w0.T, b0[None, :], wm, bm, wf, bf[None, :])


def on_device(
    thermal_departure,
    moisture_profile,
    solar_elevation_factor,
    daylight_groups,
    spreading_factor,
    entry_layer_matrix,
    entry_layer_offset,
    inner_layer_matrices,
    inner_layer_offsets,
    final_layer_matrix,
    final_layer_offset,
):
    return tuple(run(
        thermal_departure,
        moisture_profile,
        solar_elevation_factor,
        daylight_groups[:, 0],
        spreading_factor,
        entry_layer_matrix,
        entry_layer_offset,
        inner_layer_matrices,
        inner_layer_offsets,
        final_layer_matrix,
        final_layer_offset,
    ))


def solution(mesh):
    in_specs = (
        P(None, "lat", "lon"),
        P(None, "lat", "lon"),
        P("lat", "lon"),
        P("lat", "lon"),
        P("lat", "lon"),
        P(),
        P(),
        P(),
        P(),
        P(),
        P(),
    )
    out_specs = (P(None, "lat", "lon"), P(None, "lat", "lon"))
    return jax.shard_map(
        on_device, mesh=mesh, in_specs=in_specs, out_specs=out_specs, check_vma=False
    )
```

```python
import jax
import jax.numpy as jnp
from jax import lax
from jax.experimental import pallas as pl
from jax.experimental.pallas import tpu as pltpu
from jax.sharding import PartitionSpec as P

MESH = pl.DeviceIdType.MESH
GROUP = 4
EDGE = 4
CHUNKS = 2
PAD = 8


def up8(n):
    return (n + 7) // 8 * 8


def split(x):
    hi = x.astype(jnp.bfloat16)
    lo = (x - hi.astype(jnp.float32)).astype(jnp.bfloat16)
    return hi, lo


def dot(a, b):
    return jnp.dot(a, b, preferred_element_type=jnp.float32)


def dot3(w_hi, w_lo, x):
    hi, lo = split(x)
    return dot(w_hi, hi) + dot(w_hi, lo) + dot(w_lo, hi)


def gate(h):
    return h + h * jnp.tanh(h)


def roll(x, shift, axis):
    return pltpu.roll(x, shift % x.shape[axis], axis)


def kernel(
    temp, moist, mu, lit_h, spread, w0t_h, b0_h, wm_h, bm_h, wf_h, bf_h,
    heat, nxt,
    lit, w0t, b0, wm, bm, wf, bf,
    temp_v, moist_v, mu_v, spread_v, temp_r, moist_r, mu_r,
    w0_hi, w0_lo, wm_hi, wm_lo, wf_hi, wf_lo, b0_c, bm_c, bf_c,
    xs, res, res_r,
    temp_t, temp_b, spread_t, spread_b,
    pack, left_m, left_t, left_b, right_m, right_t, right_b,
    edge_0, edge_1, f_all,
    in_sem, send_sem, recv_sem, out_send, out_recv, halo_send, halo_recv,
):
    levels, rows, lanes = temp.shape
    half = rows // 2
    hid = wm_h.shape[1]
    depth = wm_h.shape[0]
    groups = half // GROUP
    lp = up8(levels)
    tiles = pack.shape[0] - 1
    slots = lanes // EDGE
    n_lat = lax.axis_size("lat")
    n_lon = lax.axis_size("lon")
    lat = lax.axis_index("lat")
    lon = lax.axis_index("lon")
    parity = lax.rem(lat, 2)
    partner = lat + 1 - 2 * parity
    mine = pl.multiple_of(parity * half, half)
    theirs = pl.multiple_of(half - parity * half, half)
    left = lax.rem(lon + n_lon - 1, n_lon)
    right = lax.rem(lon + 1, n_lon)
    has_up = lat > 0
    has_down = lat < n_lat - 1
    up = jnp.maximum(lat - 1, 0)
    down = jnp.minimum(lat + 1, n_lat - 1)

    own = [
        pltpu.make_async_copy(src, dst, in_sem.at[i])
        for i, (src, dst) in enumerate((
            (temp, temp_v), (spread, spread_v), (w0t_h, w0t), (wm_h, wm), (wf_h, wf),
            (b0_h, b0), (bm_h, bm), (bf_h, bf), (mu, mu_v), (lit_h, lit), (moist, moist_v)))
    ]
    def at(lat_to, lon_to):
        return {"lat": lat_to, "lon": lon_to}

    barrier = pltpu.get_barrier_semaphore()

    def hello(lat_to, lon_to):
        pl.semaphore_signal(barrier, inc=1, device_id=at(lat_to, lon_to), device_id_type=MESH)

    hello(lat, left)
    hello(lat, right)

    @pl.when(has_up)
    def _():
        for to in (left, lon, right):
            hello(up, to)

    @pl.when(has_down)
    def _():
        for to in (left, lon, right):
            hello(down, to)

    for copy in own:
        copy.start()

    first, last = pl.ds(0, PAD), pl.ds(rows - PAD, PAD)

    def halo(i, src, dst, lat_to, lon_to):
        return pltpu.make_async_remote_copy(
            src_ref=src, dst_ref=dst, send_sem=halo_send.at[i], recv_sem=halo_recv.at[i],
            device_id=at(lat_to, lon_to), device_id_type=MESH)

    beside = [
        halo(0, pack, right_m, lat, left),
        halo(1, pack, left_m, lat, right),
    ]
    to_up = [
        halo(2, spread.at[first, :], spread_b, up, lon),
        halo(3, temp.at[:, first, :], temp_b, up, lon),
        halo(4, pack.at[:, first, :], right_b, up, left),
        halo(5, pack.at[:, first, :], left_b, up, right),
    ]
    to_down = [
        halo(6, spread.at[last, :], spread_t, down, lon),
        halo(7, temp.at[:, last, :], temp_t, down, lon),
        halo(8, pack.at[:, last, :], right_t, down, left),
        halo(9, pack.at[:, last, :], left_t, down, right),
    ]

    for copy in own[:2]:
        copy.wait()
    lane = lax.broadcasted_iota(jnp.int32, (rows, lanes), 1)
    for t in range(tiles):
        count = min(slots, levels - t * slots)
        acc = jnp.zeros((rows, lanes), jnp.float32)
        for m in range(count):
            moved = roll(temp_v[t * slots + m], EDGE * m + 2, 1)
            acc = jnp.where(lane // EDGE == m, moved, acc)
        pack[t] = acc
    acc = jnp.where(lane < EDGE, roll(spread_v[...], 2, 1), 0.0)
    step = EDGE
    while step < lanes:
        acc = acc + roll(acc, step, 1)
        step *= 2
    pack[tiles] = acc

    @pl.when(jnp.logical_not(has_up))
    def _():
        for ref in (temp_t, spread_t, left_t, right_t):
            ref[...] = jnp.zeros_like(ref)

    @pl.when(jnp.logical_not(has_down))
    def _():
        for ref in (temp_b, spread_b, left_b, right_b):
            ref[...] = jnp.zeros_like(ref)

    for copy in own[2:]:
        copy.wait()

    xs[...] = jnp.zeros_like(xs)
    xs[0:levels, 0:hid] = w0t[0:levels, :] * 0.5
    xs[lp:lp + levels, 0:hid] = w0t[levels:2 * levels, :] * 0.5
    xs[2 * lp:2 * lp + 1, 0:hid] = w0t[2 * levels:2 * levels + 1, :] * 0.5
    w0_hi[...], w0_lo[...] = split(xs[:, 0:hid].T)
    for k in range(depth):
        wm_hi[k], wm_lo[k] = split(wm[k] * 0.5)
    wf_hi[...], wf_lo[...] = split(wf[...])

    def column(row):
        return jnp.broadcast_to(row, (lanes, row.shape[1])).T

    b0_c[...] = column(b0[...] * 0.5)
    for k in range(depth):
        bm_c[k] = column(bm[k:k + 1, :] * 0.5)
    bf_c[...] = column(bf[...])
    xs[...] = jnp.zeros_like(xs)

    pl.semaphore_wait(
        barrier, 2 + 3 * has_up.astype(jnp.int32) + 3 * has_down.astype(jnp.int32))

    chunk = half // CHUNKS

    def swap(i, src, dst):
        return pltpu.make_async_remote_copy(
            src_ref=src, dst_ref=dst, send_sem=send_sem.at[i], recv_sem=recv_sem.at[i],
            device_id=at(partner, lon), device_id_type=MESH)

    out = []
    for c in range(CHUNKS):
        theirs_c = pl.ds(pl.multiple_of(theirs + c * chunk, chunk), chunk)
        here_c = pl.ds(c * chunk, chunk)
        out.append([
            swap(3 * c, temp.at[:, theirs_c, :], temp_r.at[:, here_c, :]),
            swap(3 * c + 1, moist.at[:, theirs_c, :], moist_r.at[:, here_c, :]),
            swap(3 * c + 2, mu.at[theirs_c, :], mu_r.at[here_c, :]),
        ])

    for copy in out[0] + beside:
        copy.start()

    @pl.when(has_up)
    def _():
        for copy in to_up:
            copy.start()

    @pl.when(has_down)
    def _():
        for copy in to_down:
            copy.start()

    for later in out[1:]:
        for copy in later:
            copy.start()


    temp_f = temp_v.reshape(levels * rows, lanes)
    moist_f = moist_v.reshape(levels * rows, lanes)
    temp_rf = temp_r.reshape(levels * half, lanes)
    moist_rf = moist_r.reshape(levels * half, lanes)

    def wide(c):
        return jnp.concatenate([c] * GROUP, axis=1)

    def send(g):
        rows_g = pl.ds(g * GROUP, GROUP)
        return pltpu.make_async_remote_copy(
            src_ref=res.at[rows_g], dst_ref=res_r.at[rows_g],
            send_sem=out_send.at[g], recv_sem=out_recv.at[g],
            device_id=at(partner, lon), device_id_type=MESH)

    heat_f = heat.reshape(levels * rows, lanes)

    def place_row(r, value):
        heat_f[pl.ds(r, levels, stride=rows), :] = value * lit[r].astype(jnp.float32)

    def network(g, beside_it=lambda part: None):
        for j in range(GROUP):
            i = g * GROUP + j
            r = mine + i
            on = lit[r].astype(jnp.float32)
            off = 1.0 - on
            cols = slice(j * lanes, (j + 1) * lanes)
            xs[0:levels, cols] = (
                temp_f[pl.ds(r, levels, stride=rows), :] * on
                + temp_rf[pl.ds(i, levels, stride=half), :] * off)
            xs[lp:lp + levels, cols] = (
                moist_f[pl.ds(r, levels, stride=rows), :] * on
                + moist_rf[pl.ds(i, levels, stride=half), :] * off)
            xs[2 * lp:2 * lp + 1, cols] = (
                mu_v[pl.ds(r, 1), :] * on + mu_r[pl.ds(i, 1), :] * off)
        h = gate(dot3(w0_hi[...], w0_lo[...], xs[...]) + wide(b0_c[...]))
        beside_it(0)
        for k in range(depth):
            h = gate(dot3(wm_hi[k], wm_lo[k], h) + wide(bm_c[k]))
            beside_it(1 + k)
        y = dot3(wf_hi[...], wf_lo[...], h) + wide(bf_c[...])
        y = y * xs[2 * lp:2 * lp + 1, :]
        for j in range(GROUP):
            value = y[:, j * lanes:(j + 1) * lanes]
            res[g * GROUP + j] = value
            place_row(mine + g * GROUP + j, value)
        send(g).start()

    def arrive(c):
        for copy in out[c]:
            copy.wait()

    arrive(0)
    network(0)

    for copy in beside:
        copy.wait()

    @pl.when(has_up)
    def _():
        for copy in to_up:
            copy.wait_send()
        for copy in to_down:
            copy.wait_recv()

    @pl.when(has_down)
    def _():
        for copy in to_down:
            copy.wait_send()
        for copy in to_up:
            copy.wait_recv()

    tall = rows + 2 * PAD

    def stack(top, middle, bottom):
        return jnp.concatenate([top, middle, bottom], axis=0)

    def advance(x, f, west, east):
        beside = roll(x, 1, 0) + roll(x, x.shape[0] - 1, 0) + west + east
        return x + f * (beside - 4.0 * x)

    slot = lax.broadcasted_iota(jnp.int32, (tall, lanes), 1)
    place = lax.rem(slot, EDGE)
    zero8 = jnp.zeros((PAD, lanes), jnp.float32)

    def gather(t):
        lhs = stack(left_t[t], left_m[t], left_b[t])
        rhs = stack(right_t[t], right_m[t], right_b[t])
        here = stack(zero8, pack[t], zero8)
        return (jnp.where(place < 2, lhs, here), jnp.where(place < 2, here, rhs))

    f_west, f_east = gather(tiles)
    for t in range(tiles):
        west, east = gather(t)
        edge_0[t] = jnp.where(place == 1, roll(east, lanes - 1, 1), roll(west, 1, 1))
        west = advance(west, f_west, roll(west, 1, 1), roll(west, lanes - 1, 1))
        east = advance(east, f_east, roll(east, 1, 1), roll(east, lanes - 1, 1))
        edge_1[t] = jnp.where(place == 1, roll(east, lanes - 1, 1), roll(west, 1, 1))

    f_all[...] = stack(spread_t[...], spread_v[...], spread_b[...])
    def diffuse(k):
        t, m = k // slots, lax.rem(k, slots)
        turn = lanes - 2 - EDGE * m
        x = stack(temp_t[k], temp_v[k], temp_b[k])
        for edge in (edge_0, edge_1):
            rim = pltpu.roll(edge[t], turn, 1)
            west = jnp.where(slot == 0, rim, roll(x, 1, 1))
            east = jnp.where(slot == lanes - 1, rim, roll(x, lanes - 1, 1))
            x = advance(x, f_all[...], west, east)
        nxt[k] = x[PAD:PAD + rows]

    per = levels // (groups - 1)
    parts = depth + 1

    def both(g, carry):
        @pl.when(g == groups // CHUNKS)
        def _():
            arrive(1)

        begin = (g - 1) * per

        def some(part):
            for k in range(per * part // parts, per * (part + 1) // parts):
                diffuse(begin + k)

        network(g, some)
        return carry

    lax.fori_loop(1, groups, both, 0)
    for k in range(per * (groups - 1), levels):
        diffuse(jnp.int32(k))

    for g in range(half // GROUP):
        send(g).wait()
    for i in range(half):
        place_row(theirs + i, res_r[i])


def run(temp, moist, mu, lit, spread, w0, b0, wm, bm, wf, bf):
    levels, rows, lanes = temp.shape
    half = rows // 2
    hid = wm.shape[1]
    depth = wm.shape[0]
    lp = up8(levels)
    kp = (2 * lp + 256) // 256 * 256
    tall = rows + 2 * PAD
    tiles = (levels * EDGE + lanes - 1) // lanes
    f32, bf16 = jnp.float32, jnp.bfloat16
    vmem = pl.BlockSpec(memory_space=pltpu.VMEM)
    hbm = pl.BlockSpec(memory_space=pltpu.HBM)
    groups = half // GROUP
    dma = pltpu.SemaphoreType.DMA

    def buf(*shape, dtype=f32):
        return pltpu.VMEM(shape, dtype)

    return pl.pallas_call(
        kernel,
        out_shape=(jax.ShapeDtypeStruct(temp.shape, f32),) * 2,
        in_specs=[hbm] * 11,
        out_specs=(vmem, vmem),
        scratch_shapes=[
            pltpu.SMEM((rows,), jnp.int32), buf(*w0.T.shape), buf(1, hid), buf(*wm.shape),
            buf(*bm.shape), buf(*wf.shape), buf(1, levels),
            buf(levels, rows, lanes), buf(levels, rows, lanes), buf(rows, lanes), buf(rows, lanes),
            buf(levels, half, lanes), buf(levels, half, lanes), buf(half, lanes),
            buf(hid, kp, dtype=bf16), buf(hid, kp, dtype=bf16),
            buf(depth, hid, hid, dtype=bf16), buf(depth, hid, hid, dtype=bf16),
            buf(levels, hid, dtype=bf16), buf(levels, hid, dtype=bf16),
            buf(hid, lanes), buf(depth, hid, lanes), buf(levels, lanes),
            buf(kp, max(hid, GROUP * lanes)), buf(half, levels, lanes), buf(half, levels, lanes),
            buf(levels, PAD, lanes), buf(levels, PAD, lanes), buf(PAD, lanes), buf(PAD, lanes),
            buf(tiles + 1, rows, lanes),
            buf(tiles + 1, rows, lanes), buf(tiles + 1, PAD, lanes), buf(tiles + 1, PAD, lanes),
            buf(tiles + 1, rows, lanes), buf(tiles + 1, PAD, lanes), buf(tiles + 1, PAD, lanes),
            buf(tiles, tall, lanes), buf(tiles, tall, lanes), buf(tall, lanes),
            dma((11,)), dma((3 * CHUNKS,)), dma((3 * CHUNKS,)), dma((groups,)), dma((groups,)),
            dma((10,)), dma((10,)),
        ],
        compiler_params=pltpu.CompilerParams(
            collective_id=0, has_side_effects=True, vmem_limit_bytes=48 << 20),
    )(*(
        pltpu.with_memory_space_constraint(x, pltpu.HBM)
        for x in (temp, moist, mu, lit, spread, w0.T, b0[None, :], wm, bm, wf, bf[None, :])
    ))


def on_device(
    thermal_departure,
    moisture_profile,
    solar_elevation_factor,
    daylight_groups,
    spreading_factor,
    entry_layer_matrix,
    entry_layer_offset,
    inner_layer_matrices,
    inner_layer_offsets,
    final_layer_matrix,
    final_layer_offset,
):
    heating, state = run(
        thermal_departure,
        moisture_profile,
        solar_elevation_factor,
        daylight_groups[:, 0],
        spreading_factor,
        entry_layer_matrix,
        entry_layer_offset,
        inner_layer_matrices,
        inner_layer_offsets,
        final_layer_matrix,
        final_layer_offset,
    )
    return heating, state + heating


def solution(mesh):
    in_specs = (
        P(None, "lat", "lon"),
        P(None, "lat", "lon"),
        P("lat", "lon"),
        P("lat", "lon"),
        P("lat", "lon"),
        P(),
        P(),
        P(),
        P(),
        P(),
        P(),
    )
    out_specs = (P(None, "lat", "lon"), P(None, "lat", "lon"))
    return jax.shard_map(
        on_device, mesh=mesh, in_specs=in_specs, out_specs=out_specs, check_vma=False
    )
```

```python
import jax
import jax.numpy as jnp
from jax import lax
from jax.experimental import pallas as pl
from jax.experimental.pallas import tpu as pltpu
from jax.sharding import PartitionSpec as P

MESH = pl.DeviceIdType.MESH
GROUP = 4
EDGE = 4
CHUNKS = 2
PAD = 8


def up8(n):
    return (n + 7) // 8 * 8


def split(x):
    hi = x.astype(jnp.bfloat16)
    lo = (x - hi.astype(jnp.float32)).astype(jnp.bfloat16)
    return hi, lo


def dot(a, b):
    return jnp.dot(a, b, preferred_element_type=jnp.float32)


def dot3(w_hi, w_lo, x):
    hi, lo = split(x)
    return dot(w_hi, hi) + dot(w_hi, lo) + dot(w_lo, hi)


def gate(h):
    return h + h * jnp.tanh(h)


def roll(x, shift, axis):
    return pltpu.roll(x, shift % x.shape[axis], axis)


def kernel(
    temp, moist, mu, lit_h, spread, w0t_h, b0_h, wm_h, bm_h, wf_h, bf_h,
    heat, nxt,
    lit, w0t, b0, wm, bm, wf, bf,
    temp_v, moist_v, mu_v, spread_v, temp_r, moist_r, mu_r,
    w0_hi, w0_lo, wm_hi, wm_lo, wf_hi, wf_lo, b0_c, bm_c, bf_c,
    xs, res, res_r,
    temp_t, temp_b, spread_t, spread_b,
    pack, left_m, left_t, left_b, right_m, right_t, right_b,
    edge_0, edge_1, f_all,
    in_sem, send_sem, recv_sem, out_send, out_recv, halo_send, halo_recv,
):
    levels, rows, lanes = temp.shape
    half = rows // 2
    hid = wm_h.shape[1]
    depth = wm_h.shape[0]
    groups = half // GROUP
    lp = up8(levels)
    tiles = pack.shape[0] - 1
    slots = lanes // EDGE
    n_lat = lax.axis_size("lat")
    n_lon = lax.axis_size("lon")
    lat = lax.axis_index("lat")
    lon = lax.axis_index("lon")
    parity = lax.rem(lat, 2)
    partner = lat + 1 - 2 * parity
    mine = pl.multiple_of(parity * half, half)
    theirs = pl.multiple_of(half - parity * half, half)
    left = lax.rem(lon + n_lon - 1, n_lon)
    right = lax.rem(lon + 1, n_lon)
    has_up = lat > 0
    has_down = lat < n_lat - 1
    up = jnp.maximum(lat - 1, 0)
    down = jnp.minimum(lat + 1, n_lat - 1)

    own = [
        pltpu.make_async_copy(src, dst, in_sem.at[i])
        for i, (src, dst) in enumerate((
            (temp, temp_v), (spread, spread_v), (w0t_h, w0t), (wm_h, wm), (wf_h, wf),
            (b0_h, b0), (bm_h, bm), (bf_h, bf), (mu, mu_v), (lit_h, lit), (moist, moist_v)))
    ]
    def at(lat_to, lon_to):
        return {"lat": lat_to, "lon": lon_to}

    barrier = pltpu.get_barrier_semaphore()

    def hello(lat_to, lon_to):
        pl.semaphore_signal(barrier, inc=1, device_id=at(lat_to, lon_to), device_id_type=MESH)

    hello(lat, left)
    hello(lat, right)

    @pl.when(has_up)
    def _():
        for to in (left, lon, right):
            hello(up, to)

    @pl.when(has_down)
    def _():
        for to in (left, lon, right):
            hello(down, to)

    for copy in own:
        copy.start()

    first, last = pl.ds(0, PAD), pl.ds(rows - PAD, PAD)

    def halo(i, src, dst, lat_to, lon_to):
        return pltpu.make_async_remote_copy(
            src_ref=src, dst_ref=dst, send_sem=halo_send.at[i], recv_sem=halo_recv.at[i],
            device_id=at(lat_to, lon_to), device_id_type=MESH)

    beside = [
        halo(0, pack, right_m, lat, left),
        halo(1, pack, left_m, lat, right),
    ]
    to_up = [
        halo(2, spread.at[first, :], spread_b, up, lon),
        halo(3, temp.at[:, first, :], temp_b, up, lon),
        halo(4, pack.at[:, first, :], right_b, up, left),
        halo(5, pack.at[:, first, :], left_b, up, right),
    ]
    to_down = [
        halo(6, spread.at[last, :], spread_t, down, lon),
        halo(7, temp.at[:, last, :], temp_t, down, lon),
        halo(8, pack.at[:, last, :], right_t, down, left),
        halo(9, pack.at[:, last, :], left_t, down, right),
    ]

    for copy in own[:2]:
        copy.wait()
    lane = lax.broadcasted_iota(jnp.int32, (rows, lanes), 1)
    for t in range(tiles):
        count = min(slots, levels - t * slots)
        acc = jnp.zeros((rows, lanes), jnp.float32)
        for m in range(count):
            moved = roll(temp_v[t * slots + m], EDGE * m + 2, 1)
            acc = jnp.where(lane // EDGE == m, moved, acc)
        pack[t] = acc
    acc = jnp.where(lane < EDGE, roll(spread_v[...], 2, 1), 0.0)
    step = EDGE
    while step < lanes:
        acc = acc + roll(acc, step, 1)
        step *= 2
    pack[tiles] = acc

    @pl.when(jnp.logical_not(has_up))
    def _():
        for ref in (temp_t, spread_t, left_t, right_t):
            ref[...] = jnp.zeros_like(ref)

    @pl.when(jnp.logical_not(has_down))
    def _():
        for ref in (temp_b, spread_b, left_b, right_b):
            ref[...] = jnp.zeros_like(ref)

    for copy in own[2:]:
        copy.wait()

    xs[...] = jnp.zeros_like(xs)
    xs[0:levels, 0:hid] = w0t[0:levels, :] * 0.5
    xs[lp:lp + levels, 0:hid] = w0t[levels:2 * levels, :] * 0.5
    xs[2 * lp:2 * lp + 1, 0:hid] = w0t[2 * levels:2 * levels + 1, :] * 0.5
    w0_hi[...], w0_lo[...] = split(xs[:, 0:hid].T)
    for k in range(depth):
        wm_hi[k], wm_lo[k] = split(wm[k] * 0.5)
    wf_hi[...], wf_lo[...] = split(wf[...])

    def column(row):
        return jnp.broadcast_to(row, (lanes, row.shape[1])).T

    b0_c[...] = column(b0[...] * 0.5)
    for k in range(depth):
        bm_c[k] = column(bm[k:k + 1, :] * 0.5)
    bf_c[...] = column(bf[...])
    xs[...] = jnp.zeros_like(xs)

    pl.semaphore_wait(
        barrier, 2 + 3 * has_up.astype(jnp.int32) + 3 * has_down.astype(jnp.int32))

    chunk = half // CHUNKS

    def swap(i, src, dst):
        return pltpu.make_async_remote_copy(
            src_ref=src, dst_ref=dst, send_sem=send_sem.at[i], recv_sem=recv_sem.at[i],
            device_id=at(partner, lon), device_id_type=MESH)

    out = []
    for c in range(CHUNKS):
        theirs_c = pl.ds(pl.multiple_of(theirs + c * chunk, chunk), chunk)
        here_c = pl.ds(c * chunk, chunk)
        out.append([
            swap(3 * c, temp.at[:, theirs_c, :], temp_r.at[:, here_c, :]),
            swap(3 * c + 1, moist.at[:, theirs_c, :], moist_r.at[:, here_c, :]),
            swap(3 * c + 2, mu.at[theirs_c, :], mu_r.at[here_c, :]),
        ])

    for copy in out[0] + beside:
        copy.start()

    @pl.when(has_up)
    def _():
        for copy in to_up:
            copy.start()

    @pl.when(has_down)
    def _():
        for copy in to_down:
            copy.start()

    for later in out[1:]:
        for copy in later:
            copy.start()


    temp_f = temp_v.reshape(levels * rows, lanes)
    moist_f = moist_v.reshape(levels * rows, lanes)
    temp_rf = temp_r.reshape(levels * half, lanes)
    moist_rf = moist_r.reshape(levels * half, lanes)

    def wide(c):
        return jnp.concatenate([c] * GROUP, axis=1)

    def send(g):
        rows_g = pl.ds(g * GROUP, GROUP)
        return pltpu.make_async_remote_copy(
            src_ref=res.at[rows_g], dst_ref=res_r.at[rows_g],
            send_sem=out_send.at[g], recv_sem=out_recv.at[g],
            device_id=at(partner, lon), device_id_type=MESH)

    heat_f = heat.reshape(levels * rows, lanes)

    def place_row(r, value):
        heat_f[pl.ds(r, levels, stride=rows), :] = value * lit[r].astype(jnp.float32)

    def network(g, beside_it=lambda part: None):
        for j in range(GROUP):
            i = g * GROUP + j
            r = mine + i
            on = lit[r].astype(jnp.float32)
            off = 1.0 - on
            cols = slice(j * lanes, (j + 1) * lanes)
            xs[0:levels, cols] = (
                temp_f[pl.ds(r, levels, stride=rows), :] * on
                + temp_rf[pl.ds(i, levels, stride=half), :] * off)
            xs[lp:lp + levels, cols] = (
                moist_f[pl.ds(r, levels, stride=rows), :] * on
                + moist_rf[pl.ds(i, levels, stride=half), :] * off)
            xs[2 * lp:2 * lp + 1, cols] = (
                mu_v[pl.ds(r, 1), :] * on + mu_r[pl.ds(i, 1), :] * off)
        h = gate(dot3(w0_hi[...], w0_lo[...], xs[...]) + wide(b0_c[...]))
        beside_it(0)
        for k in range(depth):
            h = gate(dot3(wm_hi[k], wm_lo[k], h) + wide(bm_c[k]))
            beside_it(1 + k)
        y = dot3(wf_hi[...], wf_lo[...], h) + wide(bf_c[...])
        y = y * xs[2 * lp:2 * lp + 1, :]
        for j in range(GROUP):
            value = y[:, j * lanes:(j + 1) * lanes]
            res[g * GROUP + j] = value
            place_row(mine + g * GROUP + j, value)
        send(g).start()

    def arrive(c):
        for copy in out[c]:
            copy.wait()

    early = groups // CHUNKS
    arrive(0)
    for g in range(early):
        network(g)
    for c in range(1, CHUNKS):
        arrive(c)

    for copy in beside:
        copy.wait()

    @pl.when(has_up)
    def _():
        for copy in to_up:
            copy.wait_send()
        for copy in to_down:
            copy.wait_recv()

    @pl.when(has_down)
    def _():
        for copy in to_down:
            copy.wait_send()
        for copy in to_up:
            copy.wait_recv()

    tall = rows + 2 * PAD

    def stack(top, middle, bottom):
        return jnp.concatenate([top, middle, bottom], axis=0)

    def advance(x, f, west, east):
        beside = roll(x, 1, 0) + roll(x, x.shape[0] - 1, 0) + west + east
        return x + f * (beside - 4.0 * x)

    slot = lax.broadcasted_iota(jnp.int32, (tall, lanes), 1)
    place = lax.rem(slot, EDGE)
    zero8 = jnp.zeros((PAD, lanes), jnp.float32)

    def gather(t):
        lhs = stack(left_t[t], left_m[t], left_b[t])
        rhs = stack(right_t[t], right_m[t], right_b[t])
        here = stack(zero8, pack[t], zero8)
        return (jnp.where(place < 2, lhs, here), jnp.where(place < 2, here, rhs))

    f_west, f_east = gather(tiles)
    for t in range(tiles):
        west, east = gather(t)
        edge_0[t] = jnp.where(place == 1, roll(east, lanes - 1, 1), roll(west, 1, 1))
        west = advance(west, f_west, roll(west, 1, 1), roll(west, lanes - 1, 1))
        east = advance(east, f_east, roll(east, 1, 1), roll(east, lanes - 1, 1))
        edge_1[t] = jnp.where(place == 1, roll(east, lanes - 1, 1), roll(west, 1, 1))

    f_all[...] = stack(spread_t[...], spread_v[...], spread_b[...])
    def diffuse(k):
        t, m = k // slots, lax.rem(k, slots)
        turn = lanes - 2 - EDGE * m
        x = stack(temp_t[k], temp_v[k], temp_b[k])
        for edge in (edge_0, edge_1):
            rim = pltpu.roll(edge[t], turn, 1)
            west = jnp.where(slot == 0, rim, roll(x, 1, 1))
            east = jnp.where(slot == lanes - 1, rim, roll(x, lanes - 1, 1))
            x = advance(x, f_all[...], west, east)
        nxt[k] = x[PAD:PAD + rows]

    per = levels // (groups - early)
    parts = depth + 1

    def both(g, carry):
        begin = (g - early) * per

        def some(part):
            for k in range(per * part // parts, per * (part + 1) // parts):
                diffuse(begin + k)

        network(g, some)
        return carry

    lax.fori_loop(early, groups, both, 0)
    for k in range(per * (groups - early), levels):
        diffuse(jnp.int32(k))

    for g in range(half // GROUP):
        send(g).wait()
    for i in range(half):
        place_row(theirs + i, res_r[i])


def run(temp, moist, mu, lit, spread, w0, b0, wm, bm, wf, bf):
    levels, rows, lanes = temp.shape
    half = rows // 2
    hid = wm.shape[1]
    depth = wm.shape[0]
    lp = up8(levels)
    kp = (2 * lp + 256) // 256 * 256
    tall = rows + 2 * PAD
    tiles = (levels * EDGE + lanes - 1) // lanes
    f32, bf16 = jnp.float32, jnp.bfloat16
    vmem = pl.BlockSpec(memory_space=pltpu.VMEM)
    hbm = pl.BlockSpec(memory_space=pltpu.HBM)
    groups = half // GROUP
    dma = pltpu.SemaphoreType.DMA

    def buf(*shape, dtype=f32):
        return pltpu.VMEM(shape, dtype)

    return pl.pallas_call(
        kernel,
        out_shape=(jax.ShapeDtypeStruct(temp.shape, f32),) * 2,
        in_specs=[hbm] * 11,
        out_specs=(vmem, vmem),
        scratch_shapes=[
            pltpu.SMEM((rows,), jnp.int32), buf(*w0.T.shape), buf(1, hid), buf(*wm.shape),
            buf(*bm.shape), buf(*wf.shape), buf(1, levels),
            buf(levels, rows, lanes), buf(levels, rows, lanes), buf(rows, lanes), buf(rows, lanes),
            buf(levels, half, lanes), buf(levels, half, lanes), buf(half, lanes),
            buf(hid, kp, dtype=bf16), buf(hid, kp, dtype=bf16),
            buf(depth, hid, hid, dtype=bf16), buf(depth, hid, hid, dtype=bf16),
            buf(levels, hid, dtype=bf16), buf(levels, hid, dtype=bf16),
            buf(hid, lanes), buf(depth, hid, lanes), buf(levels, lanes),
            buf(kp, max(hid, GROUP * lanes)), buf(half, levels, lanes), buf(half, levels, lanes),
            buf(levels, PAD, lanes), buf(levels, PAD, lanes), buf(PAD, lanes), buf(PAD, lanes),
            buf(tiles + 1, rows, lanes),
            buf(tiles + 1, rows, lanes), buf(tiles + 1, PAD, lanes), buf(tiles + 1, PAD, lanes),
            buf(tiles + 1, rows, lanes), buf(tiles + 1, PAD, lanes), buf(tiles + 1, PAD, lanes),
            buf(tiles, tall, lanes), buf(tiles, tall, lanes), buf(tall, lanes),
            dma((11,)), dma((3 * CHUNKS,)), dma((3 * CHUNKS,)), dma((groups,)), dma((groups,)),
            dma((10,)), dma((10,)),
        ],
        compiler_params=pltpu.CompilerParams(
            collective_id=0, has_side_effects=True, vmem_limit_bytes=48 << 20),
    )(*(
        pltpu.with_memory_space_constraint(x, pltpu.HBM)
        for x in (temp, moist, mu, lit, spread, w0.T, b0[None, :], wm, bm, wf, bf[None, :])
    ))


def on_device(
    thermal_departure,
    moisture_profile,
    solar_elevation_factor,
    daylight_groups,
    spreading_factor,
    entry_layer_matrix,
    entry_layer_offset,
    inner_layer_matrices,
    inner_layer_offsets,
    final_layer_matrix,
    final_layer_offset,
):
    heating, state = run(
        thermal_departure,
        moisture_profile,
        solar_elevation_factor,
        daylight_groups[:, 0],
        spreading_factor,
        entry_layer_matrix,
        entry_layer_offset,
        inner_layer_matrices,
        inner_layer_offsets,
        final_layer_matrix,
        final_layer_offset,
    )
    return heating, state + heating


def solution(mesh):
    in_specs = (
        P(None, "lat", "lon"),
        P(None, "lat", "lon"),
        P("lat", "lon"),
        P("lat", "lon"),
        P("lat", "lon"),
        P(),
        P(),
        P(),
        P(),
        P(),
        P(),
    )
    out_specs = (P(None, "lat", "lon"), P(None, "lat", "lon"))
    return jax.shard_map(
        on_device, mesh=mesh, in_specs=in_specs, out_specs=out_specs, check_vma=False
    )
```
